32 devices in a mesh: dp: 4 (over y, x), expert: 8 (over z, core).
Axes of the slice: x: 2, y: 2, z: 4, core: 2. Of those that a mesh axis runs over, the one named last changes fastest.
Arguments:
- tokens: bfloat16 [4096, 2048], P(('dp', 'expert')), may hold values from -6 to 6
- expert_ids: int32 [4096, 4], P(('dp', 'expert')), may hold values from 0 to 7, all different within a row; in each aligned block of 128 rows (0 to 127, 128 to 255, ...) at most 80 rows name the same one
- probs: float32 [4096, 4], P(('dp', 'expert')), may hold values from 0.2 to 1
- trade: int32 [4], replicated, may hold values from 0 to 1, as said below
- gate_weight: bfloat16 [8, 2048, 768], P('expert'), may hold values from -0.125 to 0.125
- up_weight: bfloat16 [8, 2048, 768], P('expert'), may hold values from -0.125 to 0.125
- down_weight: bfloat16 [8, 768, 2048], P('expert'), may hold values from -0.21875 to 0.21875
- out_grad: bfloat16 [4096, 2048], P(('dp', 'expert')), may hold values from -0.29882812 to 0.29882812
Outputs:
- combined: bfloat16 [4096, 2048], P(('dp', 'expert'))
- gate_grad: bfloat16 [8, 2048, 768], P('expert', 'dp')
- up_grad: bfloat16 [8, 2048, 768], P('expert', 'dp')
- down_grad: bfloat16 [8, 768, 2048], P('expert', None, 'dp')
The draws below stay inside these ranges and needn't reach their ends.
Inputs may be any that keep to these rules, and one draw needn't show every extreme that they name: `trade`: index k below 4 pairs expert index k with k + 4; at least one pair trades and at least one does not. `expert_ids`: each row names 4 different experts. Within the 128 rows of one device no expert is named by more than 80 rows, a bound that some block reaches.
All inputs are finite; a program needn't handle non-finite values.
Results may differ from the reference program's by a relative error of at most 0.0095.
Values may be sent and summed in bfloat16 or wider, within the bound.
A program may use at most 128 MiB of HBM per device.

```python
import math
import jax
import jax.numpy as jnp
import numpy as np
from jax import lax

D = 2048
FF = 768
TOPK = 4
TOK_DEV = 128
EXPERTS = 8
CAP = 80
HALF = 4
ROWS = 640
TOKENS = 4096
N_DP = 4
N_EXPERT = 8


def draw_trade(key, part):
    coins = jax.random.randint(jax.random.fold_in(key, 4391), (HALF,), 0, 2, dtype=jnp.int32)
    order = jax.random.permutation(jax.random.fold_in(key, 5821), HALF)
    coins = coins.at[order[0]].set(1)
    coins = coins.at[order[1]].set(0)
    return coins.astype(jnp.int32)


def steps_of(rng, shape, split, low, top_value):
    level, own = 1.0, jax.random.fold_in(rng, 6)
    for position, blocks in split:
        steps = jnp.exp(jax.random.uniform(jax.random.fold_in(own, position), (blocks,), jnp.float32, low / len(split), top_value / len(split)))
        level = level * jnp.repeat(steps, shape[position] // blocks).reshape([-1 if axis == position else 1 for axis in range(len(shape))])
    return level


def assign_block(key, own, number, rows, amount, top, bound, skew):
    order = jax.random.permutation(key, amount)
    crowded, usual = shares(amount, rows * top, bound, skew, True), shares(amount, rows * top, bound, skew, False)
    places = jnp.arange(amount)

    def named(lengths, offset_by):
        used = int((lengths > 0).sum())
        fixed = max(1, used // 4)
        passed = fixed + (places - fixed + offset_by * (used - fixed)) % max(1, amount - fixed)
        return jnp.zeros((amount,), jnp.int32).at[order[jnp.where(places < fixed, places, passed)]].set(jnp.asarray(lengths, jnp.int32))

    lengths = jnp.where(number % 4 == 0, named(crowded, number // 4), named(usual, number - number // 4 - 1))
    mixed = jax.random.permutation(jax.random.fold_in(own, 3), amount)
    source_of, sink = mixed[0:amount // 2 * 2:2], mixed[1:amount // 2 * 2:2]
    slack = jnp.minimum(lengths[source_of] - 1, bound - lengths[sink]) // 2
    slack = jnp.where((source_of == order[0]) | (sink == order[0]) | (lengths[sink] == 0), 0, jnp.maximum(slack, 0))
    passed = jax.random.randint(jax.random.fold_in(own, 4), (amount // 2,), 0, 1 << 20) % (slack + 1)
    lengths = lengths.at[source_of].add(-passed).at[sink].add(passed)
    members = jnp.searchsorted(jnp.cumsum(lengths), jnp.arange(rows * top), side="right").astype(jnp.int32)
    listing = members.reshape(top, rows).T
    listing = listing[jax.random.permutation(jax.random.fold_in(own, 1), rows)]
    offset_by = jax.random.randint(jax.random.fold_in(own, 2), (rows, 1), 0, top)
    return jnp.take_along_axis(listing, (jnp.arange(top)[None, :] + offset_by) % top, axis=1)


def shares(number_of, total, limit, slope, full):
    portions = [(1 << 20) // math.isqrt(standing ** slope) + 1 for standing in range(1, number_of + 1)]
    largest = limit if full else min(limit, max(-(-total // number_of), total * portions[0] // sum(portions)))
    least = 1 if total - largest >= number_of - 1 else 0
    counts, rest = [largest] + [least] * (number_of - 1), total - largest - least * (number_of - 1)
    while rest > 0:
        movable = [i for i in range(1, number_of) if counts[i] < largest] or [i for i in range(1, number_of) if counts[i] < limit]
        pool, budget = sum([portions[i] for i in movable]), rest
        for i in movable:
            more = min(limit - counts[i], max(1, budget * portions[i] // pool), rest)
            counts[i] = counts[i] + more
            rest = rest - more
    return np.array(counts)


def normal_values(rng, dims, deviation, limit, cuts=(), kind=jnp.bfloat16):
    values = jax.random.normal(rng, dims, jnp.float32) * deviation
    if len(cuts) > 0:
        values = steps_of(rng, dims, cuts, -0.22, 0.18) * values
    return jnp.clip(values, min=-limit, max=limit).astype(kind)


def setup_inputs(seed: int = 0) -> dict:
    key_list = jax.random.split(jax.random.key(seed), 9)
    tokens = normal_values(key_list[0], (TOKENS, D), 1.0, 6.0, ((0, 32),))
    expert_ids_keys = jax.random.split(jax.random.fold_in(key_list[1], 1), TOKENS // TOK_DEV)
    expert_ids_turns = jax.random.permutation(jax.random.fold_in(key_list[1], 3), TOKENS // TOK_DEV)
    expert_ids = jax.vmap(lambda own, number: assign_block(jax.random.fold_in(key_list[1], 2), own, number, TOK_DEV, EXPERTS, TOPK, CAP, 2))(expert_ids_keys, expert_ids_turns).reshape((TOKENS, TOPK))
    probs = jnp.clip(0.2 + 0.8 * jax.random.uniform(key_list[2], (TOKENS, TOPK), jnp.float32) ** steps_of(key_list[2], (TOKENS, TOPK), ((0, 32),), -0.2, 0.2), 0.2, 1.0)
    trade = draw_trade(jax.random.fold_in(key_list[8], 71), 0)
    gate_weight = normal_values(key_list[4], (EXPERTS, D, FF), D ** -0.5, 0.125, ((0, 8),))
    up_weight = normal_values(key_list[5], (EXPERTS, D, FF), D ** -0.5, 0.125, ((0, 8),))
    down_weight = normal_values(key_list[6], (EXPERTS, FF, D), FF ** -0.5, 0.21875, ((0, 8),))
    out_grad = normal_values(key_list[7], (TOKENS, D), 0.05, 0.29882812, ((0, 32),))
    return {"tokens": tokens, "expert_ids": expert_ids, "probs": probs, "trade": trade, "gate_weight": gate_weight, "up_weight": up_weight, "down_weight": down_weight, "out_grad": out_grad}


def rounded(value):
    return lax.optimization_barrier(value.astype(jnp.bfloat16)).astype(jnp.float32)


def slot_numbers(expert_ids):
    sources = N_DP * N_EXPERT
    pair_count = TOK_DEV * TOPK
    chosen = expert_ids.reshape(sources, pair_count).astype(jnp.int32)
    numbers = jnp.arange(EXPERTS, dtype=jnp.int32)
    onehot = (chosen[:, :, None] == numbers[None, None, :]).astype(jnp.int32)
    earlier = jnp.cumsum(onehot, axis=1) - onehot
    placed = jnp.sum(earlier * onehot, axis=2).astype(jnp.int32)
    return (chosen * CAP + placed).astype(jnp.int32)


def reference(tokens, expert_ids, probs, trade, gate_weight, up_weight, down_weight, out_grad):
    sources = N_DP * N_EXPERT
    pair_count = TOK_DEV * TOPK
    slots = slot_numbers(expert_ids)
    pair_ids = jnp.arange(sources * pair_count, dtype=jnp.int32).reshape(sources, pair_count)
    source_ids = jnp.arange(sources, dtype=jnp.int32)[:, None]
    table = jnp.full((sources, EXPERTS * CAP), -1, jnp.int32).at[source_ids, slots].set(pair_ids)
    table = table.reshape(sources, EXPERTS, CAP).transpose(1, 0, 2).reshape(EXPERTS, sources * CAP)
    numbers = jnp.arange(EXPERTS, dtype=jnp.int32)
    halfway = EXPERTS // 2
    owners = jnp.where(trade[numbers % halfway] == 1, jnp.bitwise_xor(numbers, halfway), numbers).astype(jnp.int32)
    prob_flat = probs.reshape(-1)

    def expert_step(combined_sum, inputs):
        pairs, owner = inputs
        live = pairs >= 0
        safe_pairs = jnp.where(live, pairs, 0).astype(jnp.int32)
        token_rows = (safe_pairs // TOPK).astype(jnp.int32)
        weight_col = jnp.where(live, prob_flat[safe_pairs], jnp.zeros((), jnp.float32))
        expert_rows = jnp.where(live[:, None], tokens[token_rows], jnp.zeros((), jnp.bfloat16))
        w_gate = gate_weight[owner]
        w_up = up_weight[owner]
        w_down = down_weight[owner]
        gate_act = jnp.dot(expert_rows, w_gate, preferred_element_type=jnp.float32)
        up_act = jnp.dot(expert_rows, w_up, preferred_element_type=jnp.float32)
        sigma = jax.nn.sigmoid(gate_act)
        silu_gate = gate_act * sigma
        hidden = (silu_gate * up_act).astype(jnp.bfloat16)
        expert_out = jnp.dot(hidden, w_down, preferred_element_type=jnp.float32).astype(jnp.bfloat16)
        combined_sum = combined_sum.at[token_rows].add(weight_col[:, None] * expert_out.astype(jnp.float32))
        out_rows = (weight_col[:, None] * out_grad[token_rows].astype(jnp.float32)).astype(jnp.bfloat16)
        hidden_grad = jnp.dot(out_rows, w_down.T, preferred_element_type=jnp.float32)
        gate_back = (hidden_grad * up_act * (sigma * (1.0 + gate_act * (1.0 - sigma)))).astype(jnp.bfloat16)
        up_back = (hidden_grad * silu_gate).astype(jnp.bfloat16)
        gate_total = jnp.zeros((D, FF), jnp.float32)
        up_total = jnp.zeros((D, FF), jnp.float32)
        down_total = jnp.zeros((FF, D), jnp.float32)
        for replica in range(N_DP):
            lower = replica * ROWS
            part_rows = expert_rows[lower:lower + ROWS]
            gate_total = gate_total + rounded(jnp.dot(part_rows.T, gate_back[lower:lower + ROWS], preferred_element_type=jnp.float32))
            up_total = up_total + rounded(jnp.dot(part_rows.T, up_back[lower:lower + ROWS], preferred_element_type=jnp.float32))
            down_total = down_total + rounded(jnp.dot(hidden[lower:lower + ROWS].T, out_rows[lower:lower + ROWS], preferred_element_type=jnp.float32))
        return combined_sum, (gate_total.astype(jnp.bfloat16), up_total.astype(jnp.bfloat16), down_total.astype(jnp.bfloat16))

    combined_sum, grads = lax.scan(expert_step, jnp.zeros((TOKENS, D), jnp.float32), (table, owners))
    return (combined_sum.astype(jnp.bfloat16), grads[0][owners], grads[1][owners], grads[2][owners])
```

```python
import functools
import jax
import jax.numpy as jnp
from jax import lax
from jax.experimental import pallas as pl
from jax.experimental.pallas import tpu as pltpu
from jax.sharding import PartitionSpec as P


def sparse_local(tokens, expert_ids, probs, trade, gate_weight, up_weight, down_weight, out_grad):
    tok_count, model_width = tokens.shape
    top_count = expert_ids.shape[1]
    hidden_width = gate_weight.shape[2]
    experts = lax.axis_size("expert")
    capacity = 5 * tok_count * top_count // (4 * experts)
    halfway = experts // 2
    chosen = expert_ids.reshape(-1)
    numbers = jnp.arange(experts, dtype=jnp.int32)
    onehot = (chosen[:, None] == numbers[None, :]).astype(jnp.int32)
    earlier = jnp.cumsum(onehot, axis=0) - onehot
    slots = chosen * capacity + jnp.sum(earlier * onehot, axis=1)
    owners = jnp.where(trade[numbers % halfway] == 1, jnp.bitwise_xor(numbers, halfway), numbers)
    pair_tokens = jnp.arange(chosen.shape[0], dtype=jnp.int32) // top_count
    send_rows = (
        jnp.zeros((experts * capacity, model_width), jnp.bfloat16)
        .at[slots]
        .set(tokens[pair_tokens])
    )
    send_rows = send_rows.reshape(experts, capacity, model_width)
    out_pairs = (probs[:, :, None] * out_grad[:, None, :].astype(jnp.float32)).astype(jnp.bfloat16)
    send_grads = (
        jnp.zeros((experts * capacity, model_width), jnp.bfloat16)
        .at[slots]
        .set(out_pairs.reshape(-1, model_width))
    )
    send_grads = send_grads.reshape(experts, capacity, model_width)
    send_rows = send_rows[owners]
    send_grads = send_grads[owners]
    w_gate = gate_weight[0]
    w_up = up_weight[0]
    w_down = down_weight[0]
    arrived = lax.all_to_all(send_rows, "expert", split_axis=0, concat_axis=0, tiled=True)
    lead = arrived.shape[:2]
    flat_rows = arrived.reshape(-1, model_width)
    gate_act = jnp.dot(flat_rows, w_gate, preferred_element_type=jnp.float32)
    up_act = jnp.dot(flat_rows, w_up, preferred_element_type=jnp.float32)
    forward_hidden = (gate_act * jax.nn.sigmoid(gate_act) * up_act).astype(jnp.bfloat16)
    expert_out = jnp.dot(forward_hidden, w_down, preferred_element_type=jnp.float32).astype(
        jnp.bfloat16
    )
    arrived, expert_out, hidden, gate_act, up_act = (
        arrived,
        expert_out.reshape(lead + (model_width,)),
        forward_hidden.reshape(lead + (hidden_width,)),
        gate_act.reshape(lead + (hidden_width,)),
        up_act.reshape(lead + (hidden_width,)),
    )
    returned = lax.all_to_all(expert_out, "expert", split_axis=0, concat_axis=0, tiled=True)
    out_rows = lax.all_to_all(send_grads, "expert", split_axis=0, concat_axis=0, tiled=True)
    returned = returned[owners]
    picked = returned.reshape(-1, model_width)[slots].reshape(tok_count, top_count, model_width)
    combined = jnp.sum(probs[:, :, None] * picked.astype(jnp.float32), axis=1).astype(jnp.bfloat16)
    expert_rows = arrived.reshape(-1, model_width)
    out_rows = out_rows.reshape(-1, model_width)
    hidden = hidden.reshape(-1, hidden_width)
    gate_act = gate_act.reshape(-1, hidden_width)
    up_act = up_act.reshape(-1, hidden_width)
    hidden_grad = lax.dot_general(
        out_rows, w_down, (((1,), (1,)), ((), ())), preferred_element_type=jnp.float32
    )
    sigma = jax.nn.sigmoid(gate_act)
    gate_back = (hidden_grad * up_act * (sigma * (1.0 + gate_act * (1.0 - sigma)))).astype(
        jnp.bfloat16
    )
    up_back = (hidden_grad * (gate_act * sigma)).astype(jnp.bfloat16)
    both_back = jnp.concatenate([gate_back, up_back], axis=1)
    first = lax.dot_general(
        expert_rows, both_back, (((0,), (0,)), ((), ())), preferred_element_type=jnp.float32
    )
    second = lax.dot_general(
        out_rows, hidden, (((0,), (0,)), ((), ())), preferred_element_type=jnp.float32
    )
    summed = lax.psum_scatter(
        jnp.concatenate([first, second], axis=1).astype(jnp.bfloat16),
        "dp",
        scatter_dimension=0,
        tiled=True,
    )
    gate_part = summed[:, :hidden_width]
    up_part = summed[:, hidden_width : 2 * hidden_width]
    down_part = summed[:, 2 * hidden_width :].T
    return (combined, gate_part[None], up_part[None], down_part[None])


def layer_kernel(
    tokens, grads, weights, wg_hbm, wu_hbm, wd_hbm, combined, gate_out, up_out, down_out,
    rows, cots, wts, wg, wu, wd, wcol, hidden, back, acc, pairs, part, sib_part, far_part,
    gu, gu_far, dn, dn_far,
    load_sem, out_sem, tok_send, tok_sib, tok_recv, cot_send, cot_sib, cot_recv, wt_send, wt_recv,
    part_sib, part_sib_recv, part_send, part_recv, gu_send, gu_recv, dn_send, dn_recv,
):
    f32 = jnp.float32
    bf16 = jnp.bfloat16
    experts = lax.axis_size("expert")
    chips = experts // 2
    last = chips - 1
    replicas = lax.axis_size("dp")
    count, width = tokens.shape
    share = width // replicas
    half = share // 2
    ff = wg.shape[1]
    pair = 2 * count
    me = lax.axis_index("expert")
    z = me // 2
    c = me % 2
    d = lax.axis_index("dp")
    dx = (d // 2) * 2 + (1 - d % 2)
    dy = (1 - d // 2) * 2 + d % 2
    dd = 3 - d
    upper = z // (chips // 2)
    zm = z * (1 - upper) + (last - z) * upper
    sibling = z * 2 + (1 - c)
    inner = zm == 1
    outer = zm == 0

    def at_chip(m):
        return m * (1 - upper) + (last - m) * upper

    def source(q):
        return at_chip(jnp.where(q == 0, zm, jnp.where(q == 1, 1 - zm, q)))

    def cols_of(s, side):
        to = jnp.where(side == 0, dx, dy)
        owner = jnp.where(s == 0, dd, jnp.where(s == 3, d, to))
        h = jnp.where(s == 2, 1 - side, side)
        return pl.ds(pl.multiple_of(owner * share + h * half, half), half)

    def remote(src, dst, ssem, rsem, axis, to):
        return pltpu.make_async_remote_copy(
            src_ref=src, dst_ref=dst, send_sem=ssem, recv_sem=rsem,
            device_id={axis: to}, device_id_type=pl.DeviceIdType.MESH,
        )

    loads = [
        pltpu.make_async_copy(wg_hbm, wg, load_sem.at[0]),
        pltpu.make_async_copy(wu_hbm, wu, load_sem.at[1]),
        pltpu.make_async_copy(wd_hbm, wd, load_sem.at[2]),
        pltpu.make_async_copy(tokens, rows.at[me], load_sem.at[3]),
        pltpu.make_async_copy(weights, wts.at[me], load_sem.at[4]),
    ]

    def cot_load(p, side):
        return pltpu.make_async_copy(
            grads.at[:, cols_of(p, side)], cots.at[p, me, :, pl.ds(side * half, half)],
            load_sem.at[5 + 2 * p + side],
        )

    loads[3].start()
    loads[4].start()
    for p in range(replicas):
        for side in range(2):
            cot_load(p, side).start()
    for load in loads[:3]:
        load.start()

    barrier = pltpu.get_barrier_semaphore()
    for r in range(1, experts):
        pl.semaphore_signal(
            barrier, inc=1, device_id={"expert": (me + r) % experts},
            device_id_type=pl.DeviceIdType.MESH,
        )
    for to in (dx, dy):
        pl.semaphore_signal(
            barrier, inc=1, device_id={"dp": to}, device_id_type=pl.DeviceIdType.MESH
        )
    pl.semaphore_wait(barrier, experts + 1)

    to_chip = (at_chip(0) * 2 + c, at_chip(zm + 1) * 2 + c)
    rhalf = count // 2

    def tok_own(way, h):
        part_rows = pl.ds(h * rhalf, rhalf)
        return remote(
            tokens.at[part_rows], rows.at[me, part_rows], tok_send.at[way, z, h],
            tok_recv.at[me, h], "expert", to_chip[way],
        )

    def tok_hop(way, zp, h):
        ref = rows.at[zp * 2 + c, pl.ds(h * rhalf, rhalf)]
        return remote(
            ref, ref, tok_send.at[way, zp, h], tok_recv.at[zp * 2 + c, h], "expert", to_chip[way]
        )

    def tok_to_sib(zp):
        ref = rows.at[zp * 2 + c]
        return remote(ref, ref, tok_sib.at[zp], tok_recv.at[zp * 2 + c, 0], "expert", sibling)

    def cot_hop(way, p, zp):
        ref = cots.at[p, zp * 2 + c]
        return remote(
            ref, ref, cot_send.at[way, p, zp], cot_recv.at[p, zp * 2 + c], "expert", to_chip[way]
        )

    def cot_to_sib(p, zp):
        ref = cots.at[p, zp * 2 + c]
        return remote(ref, ref, cot_sib.at[p, zp], cot_recv.at[p, zp * 2 + c], "expert", sibling)

    def wt_copy(r):
        return remote(
            weights, wts.at[me], wt_send.at[r], wt_recv.at[me], "expert", (me + r) % experts
        )

    def wt_from(slot):
        return remote(
            weights, wts.at[slot], wt_send.at[1], wt_recv.at[slot], "expert", sibling
        )

    own_to_sib = remote(
        tokens, rows.at[me], tok_sib.at[z], tok_recv.at[me, 0], "expert", sibling
    )

    for r in range(1, experts):
        wt_copy(r).start()
    own_to_sib.start()
    for h in range(2):
        tok_own(1, h).start()
        pl.when(inner)(tok_own(0, h).start)
    for p in range(replicas):
        for side in range(2):
            cot_load(p, side).wait()
        cot_to_sib(p, z).start()

        pl.when(outer)(cot_hop(1, p, z).start)

    def part_to_sib(zp):
        return remote(
            part.at[zp * 2 + (1 - c)], sib_part.at[zp], part_sib.at[zp], part_sib_recv.at[zp],
            "expert", sibling,
        )

    eye = lax.broadcasted_iota(jnp.int32, (count, count), 0) == lax.broadcasted_iota(
        jnp.int32, (count, count), 1
    )

    def weight_column(slot):
        row = jnp.broadcast_to(wts[slot, pl.ds(me, 1), :], (count, count))
        column = jnp.sum(jnp.where(eye, row, 0.0), axis=1, keepdims=True)
        wcol[pl.ds(pl.multiple_of(slot * count, count), count), :] = jnp.broadcast_to(
            column, (count, wcol.shape[1])
        )

    loads[3].wait()
    loads[4].wait()

    @pl.loop(0, chips)
    def _(q):
        zp = source(q)
        slot = zp * 2 + c

        @pl.when(jnp.logical_and(q > 0, jnp.logical_not(jnp.logical_and(inner, q == 2))))
        def _():
            @pl.when(jnp.logical_not(jnp.logical_and(inner, q == 3)))
            def _():
                tok_hop(0, zp, 0).wait_recv()

                @pl.when(inner)
                def _():
                    tok_hop(1, zp, 0).start()
                    tok_hop(0, at_chip(2), 0).wait_recv()
                    tok_hop(0, at_chip(2), 0).start()

            tok_hop(0, zp, 1).wait_recv()

            @pl.when(jnp.logical_and(inner, q == 1))
            def _():
                tok_hop(1, zp, 1).start()
                tok_hop(0, at_chip(2), 1).wait_recv()
                tok_hop(0, at_chip(2), 1).start()
                tok_to_sib(at_chip(2)).start()

            @pl.when(jnp.logical_and(inner, q == 3))
            def _():
                tok_hop(0, zp, 1).start()
                cot_hop(0, 0, z).start()

            tok_to_sib(zp).start()

        @pl.when(jnp.logical_and(inner, q == 2))
        def _():
            for p in range(replicas):
                cot_hop(1, p, z).start()
                cot_hop(1, p, at_chip(0)).wait_recv()
                cot_hop(1, p, at_chip(0)).start()
            tok_hop(0, at_chip(3), 0).wait_recv()
            tok_hop(0, at_chip(3), 0).start()

        @pl.when(q == 0)
        def _():
            wt_from(sibling).wait_recv()
            weight_column(me)
            weight_column(sibling)
            for load in loads[:3]:
                load.wait()

        @pl.when(q > 0)
        def _():
            for k in range(2):
                wt_from(zp * 2 + k).wait_recv()
                weight_column(zp * 2 + k)

        remote(
            rows.at[zp * 2 + 1 - c], rows.at[zp * 2 + 1 - c], tok_sib.at[zp],
            tok_recv.at[zp * 2 + 1 - c, 0], "expert", sibling,
        ).wait_recv()
        where = pl.ds(pl.multiple_of(zp * pair, pair), pair)
        x = rows[pl.ds(zp * 2, 2)].reshape(pair, width)
        tile = ff // 3

        @pl.loop(0, 3)
        def _(n):
            cols = pl.ds(pl.multiple_of(n * tile, tile), tile)
            g = jnp.dot(x, wg[:, cols], preferred_element_type=f32)
            u = jnp.dot(x, wu[:, cols], preferred_element_type=f32)
            sigma = jax.nn.sigmoid(g)
            silu = g * sigma
            hidden[where, cols] = (silu * u).astype(bf16)
            back[where, cols] = (u * (sigma * (1.0 + g * (1.0 - sigma)))).astype(bf16)
            back[where, pl.ds(pl.multiple_of(ff + n * tile, tile), tile)] = silu.astype(bf16)

        @pl.loop(0, replicas)
        def _(n):
            cols = pl.ds(pl.multiple_of(n * share, share), share)
            o = jnp.dot(hidden[where, :], wd[:, cols], preferred_element_type=f32)
            o = (o * wcol[where, 0:1]).astype(bf16)
            part[zp * 2, :, cols] = o[:count]
            part[zp * 2 + 1, :, cols] = o[count:]

        part_to_sib(zp).start()

    def part_copy(m):
        zp = at_chip(m)
        return remote(
            part.at[zp * 2 + c], far_part.at[z], part_send.at[m], part_recv.at[z], "expert",
            zp * 2 + c,
        )

    def dn_copy(s, side):
        return remote(
            dn.at[s, side], dn_far.at[side, s], dn_send.at[s, side], dn_recv.at[side, s], "dp",
            (dx, dy)[side],
        )

    def down_grad(p):
        for side in range(2):
            dn[p, side] = lax.dot_general(
                hidden[...], pairs[:, side * half:(side + 1) * half], (((0,), (0,)), ((), ())),
                preferred_element_type=f32,
            ).astype(bf16)

    def add(a, b):
        return (a.astype(f32) + b.astype(f32)).astype(bf16)

    @pl.loop(0, replicas)
    def _(p):
        def use(q):
            zp = source(q)
            other = zp * 2 + 1 - c
            remote(
                cots.at[p, other], cots.at[p, other], cot_sib.at[p, zp], cot_recv.at[p, other],
                "expert", sibling,
            ).wait_recv()
            where = pl.ds(pl.multiple_of(zp * pair, pair), pair)
            both = cots[p, pl.ds(zp * 2, 2)].reshape(pair, share)
            scaled = (wcol[where, 0:1] * both.astype(f32)).astype(bf16)
            pairs[where, :] = scaled
            more = lax.dot_general(
                scaled,
                jnp.concatenate([wd[:, cols_of(p, 0)], wd[:, cols_of(p, 1)]], axis=1),
                (((1,), (1,)), ((), ())), preferred_element_type=f32,
            )
            total = jnp.where(p == 0, more, acc[where, :] + more)
            acc[where, :] = total

            @pl.when(p == replicas - 1)
            def _():
                for n in range(2):
                    cols = slice(n * ff, (n + 1) * ff)
                    back[where, cols] = (acc[where, :] * back[where, cols].astype(f32)).astype(bf16)

        for q in range(chips):
            zp = source(q)
            if q == 1:
                pl.when(outer)(cot_hop(0, p, zp).wait_recv)
            elif q > 1:
                cot_hop(0, p, zp).wait_recv()
                pl.when(inner)(cot_hop(0, p, zp).start)
            if q > 0:
                cot_to_sib(p, zp).start()
            if q == last:

                @pl.when(jnp.logical_and(inner, p < replicas - 1))
                def _():
                    cot_hop(0, p + 1, z).start()

            if q > 0:
                use(q - 1)
        use(last)

        @pl.when(p < replicas - 1)
        def _():
            down_grad(p)

        for s in range(3):

            @pl.when(p == s)
            def _():
                for side in range(2):
                    if s == 2:
                        dn_copy(0, 1 - side).wait_recv()
                        dn[2, side] = add(dn[2, side], dn_far[1 - side, 0])
                    dn_copy(s, side).start()

        @pl.when(p == 0)
        def _():
            for zp in range(chips):
                remote(
                    part.at[zp * 2 + (1 - c)], sib_part.at[zp], part_sib.at[zp],
                    part_sib_recv.at[zp], "expert", sibling,
                ).wait_recv()
                part[zp * 2 + c] = add(part[zp * 2 + c], sib_part[zp])

        @pl.when(p == replicas - 2)
        def _():
            pl.when(inner)(part_copy(2).start)

    @pl.when(inner)
    def _():
        part_copy(0).start()

    @pl.when(outer)
    def _():
        for m in (1, 2, 3):
            part_copy(m).start()

    def gu_copy(s, side, n):
        to = jnp.where(side == 0, dx, dy)
        return remote(
            gu.at[s, side, n], gu_far.at[side, s, n], gu_send.at[s, side, n],
            gu_recv.at[side, s, n], "dp", to,
        )

    @pl.loop(0, 4 * replicas)
    def _(k):
        s = k // 4
        n = (k // 2) % 2
        side = k % 2
        lhs = rows[:, :, cols_of(s, side)].reshape(experts * count, half)
        gu[s, side, n] = lax.dot_general(
            lhs, back[:, pl.ds(pl.multiple_of(n * ff, ff), ff)], (((0,), (0,)), ((), ())),
            preferred_element_type=f32,
        ).astype(bf16)

        @pl.when(s == 2)
        def _():
            gu_copy(0, 1 - side, n).wait_recv()
            gu[2, side, n] = add(gu[2, side, n], gu_far[1 - side, 0, n])

        @pl.when(s < 3)
        def _():
            gu_copy(s, side, n).start()

    pl.when(inner)(part_copy(3).start)
    down_grad(replicas - 1)

    def total(own, one, two):
        return (own.astype(f32) + one.astype(f32) + two.astype(f32)).astype(bf16)

    def down_store(side):
        return pltpu.make_async_copy(
            dn.at[3, side], down_out.at[:, pl.ds(side * half, half)], out_sem.at[side]
        )

    for side in range(2):
        dn_copy(1, side).wait_recv()
        dn_copy(2, 1 - side).wait_recv()
        dn[3, side] = total(dn[3, side], dn_far[side, 1], dn_far[1 - side, 2])
        down_store(side).start()

    def far_copy(m):
        zp = at_chip(m)
        return remote(
            part.at[zp * 2 + c], far_part.at[zp], part_send.at[m], part_recv.at[zp], "expert",
            zp * 2 + c,
        )

    for m in range(chips):
        pl.when(zm != m)(far_copy(m).wait_recv)
    mixed = part[me].astype(f32)
    for q in range(1, chips):
        mixed = mixed + far_part[source(q)].astype(f32)
    part[me] = mixed.astype(bf16)
    mixed_store = pltpu.make_async_copy(part.at[me], combined, out_sem.at[2])
    mixed_store.start()

    def gu_store(side, n):
        return pltpu.make_async_copy(
            gu.at[3, side, n], (gate_out, up_out)[n].at[pl.ds(side * half, half)],
            out_sem.at[3 + 2 * n + side],
        )

    for n in range(2):
        for side in range(2):
            gu_copy(1, side, n).wait_recv()
            gu_copy(2, 1 - side, n).wait_recv()
            gu[3, side, n] = total(gu[3, side, n], gu_far[side, 1, n], gu_far[1 - side, 2, n])
            gu_store(side, n).start()

    own_to_sib.wait_send()
    for h in range(2):
        tok_own(1, h).wait_send()

        @pl.when(inner)
        def _():
            tok_own(0, h).wait_send()
            tok_hop(1, at_chip(0), h).wait_send()
            tok_hop(0, at_chip(2), h).wait_send()
            tok_hop(0, at_chip(3), h).wait_send()

    for p in range(replicas):
        cot_hop(1, p, z).wait_send()

        @pl.when(inner)
        def _():
            cot_hop(0, p, z).wait_send()
            cot_hop(1, p, at_chip(0)).wait_send()
            cot_hop(0, p, at_chip(2)).wait_send()
            cot_hop(0, p, at_chip(3)).wait_send()

    for r in range(1, experts):
        wt_copy(r).wait_send()
    for q in range(chips):
        zp = source(q)
        if q > 0:
            tok_to_sib(zp).wait_send()
        part_to_sib(zp).wait_send()
        for p in range(replicas):
            cot_to_sib(p, zp).wait_send()
        pl.when(zm != q)(part_copy(q).wait_send)
    for s in range(3):
        for side in range(2):
            dn_copy(s, side).wait_send()
            for n in range(2):
                gu_copy(s, side, n).wait_send()
    for side in range(2):
        down_store(side).wait()
        for n in range(2):
            gu_store(side, n).wait()
    mixed_store.wait()


def chain_local(tokens, expert_ids, probs, trade, gate_weight, up_weight, down_weight, out_grad):
    count, width = tokens.shape
    ff = gate_weight.shape[2]
    experts = lax.axis_size("expert")
    replicas = lax.axis_size("dp")
    chips = experts // 2
    share = width // replicas
    half = share // 2
    halfway = experts // 2
    numbers = jnp.arange(experts, dtype=jnp.int32)
    owners = jnp.where(
        jnp.concatenate([trade, trade]) == 1, jnp.bitwise_xor(numbers, halfway), numbers
    )
    weights = jnp.sum(
        jnp.where(expert_ids.T[None] == owners[:, None, None], probs.T[None], 0.0), axis=1
    )
    bf16, f32 = jnp.bfloat16, jnp.float32
    dma = pltpu.SemaphoreType.DMA
    total = experts * count
    hbm = pl.BlockSpec(memory_space=pl.ANY)
    combined, gate, up, down = pl.pallas_call(
        layer_kernel,
        out_shape=(
            jax.ShapeDtypeStruct((count, width), bf16),
            jax.ShapeDtypeStruct((share, ff), bf16),
            jax.ShapeDtypeStruct((share, ff), bf16),
            jax.ShapeDtypeStruct((ff, share), bf16),
        ),
        in_specs=[hbm] * 6,
        out_specs=(hbm,) * 4,
        scratch_shapes=[
            pltpu.VMEM((experts, count, width), bf16),
            pltpu.VMEM((replicas, experts, count, share), bf16),
            pltpu.VMEM((experts, experts, count), f32),
            pltpu.VMEM((width, ff), bf16),
            pltpu.VMEM((width, ff), bf16),
            pltpu.VMEM((ff, width), bf16),
            pltpu.VMEM((total, count), f32),
            pltpu.VMEM((total, ff), bf16),
            pltpu.VMEM((total, 2 * ff), bf16),
            pltpu.VMEM((total, ff), f32),
            pltpu.VMEM((total, share), bf16),
            pltpu.VMEM((experts, count, width), bf16),
            pltpu.VMEM((chips, count, width), bf16),
            pltpu.VMEM((chips, count, width), bf16),
            pltpu.VMEM((4, 2, 2, half, ff), bf16),
            pltpu.VMEM((2, 3, 2, half, ff), bf16),
            pltpu.VMEM((4, 2, ff, half), bf16),
            pltpu.VMEM((2, 3, ff, half), bf16),
            dma((5 + 2 * replicas,)),
            dma((7,)),
            dma((2, chips, 2)),
            dma((chips,)),
            dma((experts, 2)),
            dma((2, replicas, chips)),
            dma((replicas, chips)),
            dma((replicas, experts)),
            dma((experts,)),
            dma((experts,)),
            dma((chips,)),
            dma((chips,)),
            dma((chips,)),
            dma((chips,)),
            dma((3, 2, 2)),
            dma((2, 3, 2)),
            dma((3, 2)),
            dma((2, 3)),
        ],
        compiler_params=pltpu.CompilerParams(
            collective_id=0, has_side_effects=True, vmem_limit_bytes=67043328
        ),
    )(tokens, out_grad, weights, gate_weight[0], up_weight[0], down_weight[0])
    return combined, gate[None], up[None], down[None]


def local(tokens, expert_ids, *rest):
    experts, replicas = lax.axis_size("expert"), lax.axis_size("dp")
    capacity = 5 * tokens.shape[0] * expert_ids.shape[1] // (4 * experts)
    if tokens.shape[0] <= 2 * capacity and experts == 8 and replicas == 4:
        return chain_local(tokens, expert_ids, *rest)
    return sparse_local(tokens, expert_ids, *rest)


def solution(mesh):
    return jax.shard_map(
        local,
        mesh=mesh,
        in_specs=(
            P(("dp", "expert"), None),
            P(("dp", "expert"), None),
            P(("dp", "expert"), None),
            P(),
            P("expert", None, None),
            P("expert", None, None),
            P("expert", None, None),
            P(("dp", "expert"), None),
        ),
        out_specs=(
            P(("dp", "expert"), None),
            P("expert", "dp", None),
            P("expert", "dp", None),
            P("expert", None, "dp"),
        ),
        check_vma=False,
    )
```

```python
import functools
import jax
import jax.numpy as jnp
from jax import lax
from jax.experimental import pallas as pl
from jax.experimental.pallas import tpu as pltpu
from jax.sharding import PartitionSpec as P


def sparse_local(tokens, expert_ids, probs, trade, gate_weight, up_weight, down_weight, out_grad):
    tok_count, model_width = tokens.shape
    top_count = expert_ids.shape[1]
    hidden_width = gate_weight.shape[2]
    experts = lax.axis_size("expert")
    capacity = 5 * tok_count * top_count // (4 * experts)
    halfway = experts // 2
    chosen = expert_ids.reshape(-1)
    numbers = jnp.arange(experts, dtype=jnp.int32)
    onehot = (chosen[:, None] == numbers[None, :]).astype(jnp.int32)
    earlier = jnp.cumsum(onehot, axis=0) - onehot
    slots = chosen * capacity + jnp.sum(earlier * onehot, axis=1)
    owners = jnp.where(trade[numbers % halfway] == 1, jnp.bitwise_xor(numbers, halfway), numbers)
    pair_tokens = jnp.arange(chosen.shape[0], dtype=jnp.int32) // top_count
    send_rows = (
        jnp.zeros((experts * capacity, model_width), jnp.bfloat16)
        .at[slots]
        .set(tokens[pair_tokens])
    )
    send_rows = send_rows.reshape(experts, capacity, model_width)
    out_pairs = (probs[:, :, None] * out_grad[:, None, :].astype(jnp.float32)).astype(jnp.bfloat16)
    send_grads = (
        jnp.zeros((experts * capacity, model_width), jnp.bfloat16)
        .at[slots]
        .set(out_pairs.reshape(-1, model_width))
    )
    send_grads = send_grads.reshape(experts, capacity, model_width)
    send_rows = send_rows[owners]
    send_grads = send_grads[owners]
    w_gate = gate_weight[0]
    w_up = up_weight[0]
    w_down = down_weight[0]
    arrived = lax.all_to_all(send_rows, "expert", split_axis=0, concat_axis=0, tiled=True)
    lead = arrived.shape[:2]
    flat_rows = arrived.reshape(-1, model_width)
    gate_act = jnp.dot(flat_rows, w_gate, preferred_element_type=jnp.float32)
    up_act = jnp.dot(flat_rows, w_up, preferred_element_type=jnp.float32)
    forward_hidden = (gate_act * jax.nn.sigmoid(gate_act) * up_act).astype(jnp.bfloat16)
    expert_out = jnp.dot(forward_hidden, w_down, preferred_element_type=jnp.float32).astype(
        jnp.bfloat16
    )
    arrived, expert_out, hidden, gate_act, up_act = (
        arrived,
        expert_out.reshape(lead + (model_width,)),
        forward_hidden.reshape(lead + (hidden_width,)),
        gate_act.reshape(lead + (hidden_width,)),
        up_act.reshape(lead + (hidden_width,)),
    )
    returned = lax.all_to_all(expert_out, "expert", split_axis=0, concat_axis=0, tiled=True)
    out_rows = lax.all_to_all(send_grads, "expert", split_axis=0, concat_axis=0, tiled=True)
    returned = returned[owners]
    picked = returned.reshape(-1, model_width)[slots].reshape(tok_count, top_count, model_width)
    combined = jnp.sum(probs[:, :, None] * picked.astype(jnp.float32), axis=1).astype(jnp.bfloat16)
    expert_rows = arrived.reshape(-1, model_width)
    out_rows = out_rows.reshape(-1, model_width)
    hidden = hidden.reshape(-1, hidden_width)
    gate_act = gate_act.reshape(-1, hidden_width)
    up_act = up_act.reshape(-1, hidden_width)
    hidden_grad = lax.dot_general(
        out_rows, w_down, (((1,), (1,)), ((), ())), preferred_element_type=jnp.float32
    )
    sigma = jax.nn.sigmoid(gate_act)
    gate_back = (hidden_grad * up_act * (sigma * (1.0 + gate_act * (1.0 - sigma)))).astype(
        jnp.bfloat16
    )
    up_back = (hidden_grad * (gate_act * sigma)).astype(jnp.bfloat16)
    both_back = jnp.concatenate([gate_back, up_back], axis=1)
    first = lax.dot_general(
        expert_rows, both_back, (((0,), (0,)), ((), ())), preferred_element_type=jnp.float32
    )
    second = lax.dot_general(
        out_rows, hidden, (((0,), (0,)), ((), ())), preferred_element_type=jnp.float32
    )
    summed = lax.psum_scatter(
        jnp.concatenate([first, second], axis=1).astype(jnp.bfloat16),
        "dp",
        scatter_dimension=0,
        tiled=True,
    )
    gate_part = summed[:, :hidden_width]
    up_part = summed[:, hidden_width : 2 * hidden_width]
    down_part = summed[:, 2 * hidden_width :].T
    return (combined, gate_part[None], up_part[None], down_part[None])


def layer_kernel(
    tokens, grads, ids, probs, trade, wg_hbm, wu_hbm, wd_hbm,
    combined, gate_out, up_out, down_out,
    rows, cots, all_ids, all_probs, wg, wu, wd, wcol, hidden, back, acc, pairs, part, sib_part, far_part,
    gu, gu_far, dn, dn_far,
    load_sem, out_sem, tok_send, tok_sib, tok_recv, cot_send, cot_sib, cot_recv, wt_send, wt_recv,
    part_sib, part_sib_recv, part_send, part_recv, gu_send, gu_recv, dn_send, dn_recv,
):
    f32 = jnp.float32
    bf16 = jnp.bfloat16
    experts = lax.axis_size("expert")
    chips = experts // 2
    last = chips - 1
    replicas = lax.axis_size("dp")
    count, width = tokens.shape
    share = width // replicas
    half = share // 2
    ff = wg.shape[1]
    pair = 2 * count
    me = lax.axis_index("expert")
    z = me // 2
    c = me % 2
    d = lax.axis_index("dp")
    dx = (d // 2) * 2 + (1 - d % 2)
    dy = (1 - d // 2) * 2 + d % 2
    dd = 3 - d
    upper = z // (chips // 2)
    zm = z * (1 - upper) + (last - z) * upper
    sibling = z * 2 + (1 - c)
    inner = zm == 1
    outer = zm == 0

    def at_chip(m):
        return m * (1 - upper) + (last - m) * upper

    def source(q):
        return at_chip(jnp.where(q == 0, zm, jnp.where(q == 1, 1 - zm, q)))

    def cols_of(s, side):
        to = jnp.where(side == 0, dx, dy)
        owner = jnp.where(s == 0, dd, jnp.where(s == 3, d, to))
        h = jnp.where(s == 2, 1 - side, side)
        return pl.ds(pl.multiple_of(owner * share + h * half, half), half)

    def remote(src, dst, ssem, rsem, axis, to):
        return pltpu.make_async_remote_copy(
            src_ref=src, dst_ref=dst, send_sem=ssem, recv_sem=rsem,
            device_id={axis: to}, device_id_type=pl.DeviceIdType.MESH,
        )

    loads = [
        pltpu.make_async_copy(wg_hbm, wg, load_sem.at[0]),
        pltpu.make_async_copy(wu_hbm, wu, load_sem.at[1]),
        pltpu.make_async_copy(wd_hbm, wd, load_sem.at[2]),
        pltpu.make_async_copy(tokens, rows.at[me], load_sem.at[3]),
        pltpu.make_async_copy(ids, all_ids.at[me], load_sem.at[4]),
        pltpu.make_async_copy(probs, all_probs.at[me], load_sem.at[5]),
    ]

    def cot_load(p, side):
        return pltpu.make_async_copy(
            grads.at[:, cols_of(p, side)], cots.at[p, me, :, pl.ds(side * half, half)],
            load_sem.at[6 + 2 * p + side],
        )

    for load in loads[3:]:
        load.start()
    for p in range(replicas):
        for side in range(2):
            cot_load(p, side).start()
    for load in loads[:3]:
        load.start()

    barrier = pltpu.get_barrier_semaphore()
    for r in range(1, experts):
        pl.semaphore_signal(
            barrier, inc=1, device_id={"expert": (me + r) % experts},
            device_id_type=pl.DeviceIdType.MESH,
        )
    for to in (dx, dy):
        pl.semaphore_signal(
            barrier, inc=1, device_id={"dp": to}, device_id_type=pl.DeviceIdType.MESH
        )
    pl.semaphore_wait(barrier, experts + 1)

    to_chip = (at_chip(0) * 2 + c, at_chip(zm + 1) * 2 + c)
    rhalf = count // 2

    def tok_own(way, h):
        part_rows = pl.ds(h * rhalf, rhalf)
        return remote(
            tokens.at[part_rows], rows.at[me, part_rows], tok_send.at[way, z, h],
            tok_recv.at[me, h], "expert", to_chip[way],
        )

    def tok_hop(way, zp, h):
        ref = rows.at[zp * 2 + c, pl.ds(h * rhalf, rhalf)]
        return remote(
            ref, ref, tok_send.at[way, zp, h], tok_recv.at[zp * 2 + c, h], "expert", to_chip[way]
        )

    def tok_to_sib(zp):
        ref = rows.at[zp * 2 + c]
        return remote(ref, ref, tok_sib.at[zp], tok_recv.at[zp * 2 + c, 0], "expert", sibling)

    def cot_hop(way, p, zp):
        ref = cots.at[p, zp * 2 + c]
        return remote(
            ref, ref, cot_send.at[way, p, zp], cot_recv.at[p, zp * 2 + c], "expert", to_chip[way]
        )

    def cot_to_sib(p, zp):
        ref = cots.at[p, zp * 2 + c]
        return remote(ref, ref, cot_sib.at[p, zp], cot_recv.at[p, zp * 2 + c], "expert", sibling)

    def route_copy(r, k):
        ref, dst = ((ids, all_ids), (probs, all_probs))[k]
        return remote(
            ref, dst.at[me], wt_send.at[k, r], wt_recv.at[k, me], "expert", (me + r) % experts
        )

    def route_from(slot, k):
        ref, dst = ((ids, all_ids), (probs, all_probs))[k]
        return remote(
            ref, dst.at[slot], wt_send.at[k, 1], wt_recv.at[k, slot], "expert", sibling
        )

    own_to_sib = remote(
        tokens, rows.at[me], tok_sib.at[z], tok_recv.at[me, 0], "expert", sibling
    )

    for r in range(1, experts):
        for k in range(2):
            route_copy(r, k).start()
    own_to_sib.start()
    for h in range(2):
        tok_own(1, h).start()
        pl.when(inner)(tok_own(0, h).start)
    for p in range(replicas):
        for side in range(2):
            cot_load(p, side).wait()
        cot_to_sib(p, z).start()

        pl.when(outer)(cot_hop(1, p, z).start)

    def part_to_sib(zp):
        return remote(
            part.at[zp * 2 + (1 - c)], sib_part.at[zp], part_sib.at[zp], part_sib_recv.at[zp],
            "expert", sibling,
        )

    eye = lax.broadcasted_iota(jnp.int32, (count, count), 0) == lax.broadcasted_iota(
        jnp.int32, (count, count), 1
    )

    halfway = experts // 2
    swapped = jnp.where(me < halfway, me + halfway, me - halfway)
    name = jnp.where(trade[me % halfway] == 1, swapped, me)

    def weight_column(slot):
        row = jnp.sum(
            jnp.where(all_ids[slot] == name, all_probs[slot], 0.0), axis=0, keepdims=True
        )
        row = jnp.broadcast_to(row, (count, count))
        column = jnp.sum(jnp.where(eye, row, 0.0), axis=1, keepdims=True)
        wcol[pl.ds(pl.multiple_of(slot * count, count), count), :] = jnp.broadcast_to(
            column, (count, wcol.shape[1])
        )

    for load in loads[3:]:
        load.wait()

    @pl.loop(0, chips)
    def _(q):
        zp = source(q)
        slot = zp * 2 + c

        @pl.when(jnp.logical_and(q > 0, jnp.logical_not(jnp.logical_and(inner, q == 2))))
        def _():
            @pl.when(jnp.logical_not(jnp.logical_and(inner, q == 3)))
            def _():
                tok_hop(0, zp, 0).wait_recv()

                @pl.when(inner)
                def _():
                    tok_hop(1, zp, 0).start()
                    tok_hop(0, at_chip(2), 0).wait_recv()
                    tok_hop(0, at_chip(2), 0).start()

            tok_hop(0, zp, 1).wait_recv()

            @pl.when(jnp.logical_and(inner, q == 1))
            def _():
                tok_hop(1, zp, 1).start()
                tok_hop(0, at_chip(2), 1).wait_recv()
                tok_hop(0, at_chip(2), 1).start()
                tok_to_sib(at_chip(2)).start()

            @pl.when(jnp.logical_and(inner, q == 3))
            def _():
                tok_hop(0, zp, 1).start()
                cot_hop(0, 0, z).start()

            tok_to_sib(zp).start()

        @pl.when(jnp.logical_and(inner, q == 2))
        def _():
            for p in range(replicas):
                cot_hop(1, p, z).start()
                cot_hop(1, p, at_chip(0)).wait_recv()
                cot_hop(1, p, at_chip(0)).start()
            tok_hop(0, at_chip(3), 0).wait_recv()
            tok_hop(0, at_chip(3), 0).start()

        @pl.when(q == 0)
        def _():
            for k in range(2):
                route_from(sibling, k).wait_recv()
            weight_column(me)
            weight_column(sibling)
            for load in loads[:3]:
                load.wait()

        @pl.when(q > 0)
        def _():
            for k in range(2):
                for part_of in range(2):
                    route_from(zp * 2 + k, part_of).wait_recv()
                weight_column(zp * 2 + k)

        remote(
            rows.at[zp * 2 + 1 - c], rows.at[zp * 2 + 1 - c], tok_sib.at[zp],
            tok_recv.at[zp * 2 + 1 - c, 0], "expert", sibling,
        ).wait_recv()
        where = pl.ds(pl.multiple_of(zp * pair, pair), pair)
        x = rows[pl.ds(zp * 2, 2)].reshape(pair, width)
        tile = ff // 3

        @pl.loop(0, 3)
        def _(n):
            cols = pl.ds(pl.multiple_of(n * tile, tile), tile)
            g = jnp.dot(x, wg[:, cols], preferred_element_type=f32)
            u = jnp.dot(x, wu[:, cols], preferred_element_type=f32)
            sigma = jax.nn.sigmoid(g)
            silu = g * sigma
            hidden[where, cols] = (silu * u).astype(bf16)
            back[where, cols] = (u * (sigma * (1.0 + g * (1.0 - sigma)))).astype(bf16)
            back[where, pl.ds(pl.multiple_of(ff + n * tile, tile), tile)] = silu.astype(bf16)

        @pl.loop(0, replicas)
        def _(n):
            cols = pl.ds(pl.multiple_of(n * share, share), share)
            o = jnp.dot(hidden[where, :], wd[:, cols], preferred_element_type=f32)
            o = (o * wcol[where, 0:1]).astype(bf16)
            part[zp * 2, :, cols] = o[:count]
            part[zp * 2 + 1, :, cols] = o[count:]

        part_to_sib(zp).start()

    def part_copy(m):
        zp = at_chip(m)
        return remote(
            part.at[zp * 2 + c], far_part.at[z], part_send.at[m], part_recv.at[z], "expert",
            zp * 2 + c,
        )

    def dn_copy(s, side):
        return remote(
            dn.at[s, side], dn_far.at[side, s], dn_send.at[s, side], dn_recv.at[side, s], "dp",
            (dx, dy)[side],
        )

    def down_grad(p):
        for side in range(2):
            dn[p, side] = lax.dot_general(
                hidden[...], pairs[:, side * half:(side + 1) * half], (((0,), (0,)), ((), ())),
                preferred_element_type=f32,
            ).astype(bf16)

    def add(a, b):
        return (a.astype(f32) + b.astype(f32)).astype(bf16)

    @pl.loop(0, replicas)
    def _(p):
        def use(q):
            zp = source(q)
            other = zp * 2 + 1 - c
            remote(
                cots.at[p, other], cots.at[p, other], cot_sib.at[p, zp], cot_recv.at[p, other],
                "expert", sibling,
            ).wait_recv()
            where = pl.ds(pl.multiple_of(zp * pair, pair), pair)
            both = cots[p, pl.ds(zp * 2, 2)].reshape(pair, share)
            scaled = (wcol[where, 0:1] * both.astype(f32)).astype(bf16)
            pairs[where, :] = scaled
            more = lax.dot_general(
                scaled,
                jnp.concatenate([wd[:, cols_of(p, 0)], wd[:, cols_of(p, 1)]], axis=1),
                (((1,), (1,)), ((), ())), preferred_element_type=f32,
            )
            total = jnp.where(p == 0, more, acc[where, :] + more)
            acc[where, :] = total

            @pl.when(p == replicas - 1)
            def _():
                for n in range(2):
                    cols = slice(n * ff, (n + 1) * ff)
                    back[where, cols] = (acc[where, :] * back[where, cols].astype(f32)).astype(bf16)

        for q in range(chips):
            zp = source(q)
            if q == 1:
                pl.when(outer)(cot_hop(0, p, zp).wait_recv)
            elif q > 1:
                cot_hop(0, p, zp).wait_recv()
                pl.when(inner)(cot_hop(0, p, zp).start)
            if q > 0:
                cot_to_sib(p, zp).start()
            if q == last:

                @pl.when(jnp.logical_and(inner, p < replicas - 1))
                def _():
                    cot_hop(0, p + 1, z).start()

            if q > 0:
                use(q - 1)
        use(last)

        @pl.when(p < replicas - 1)
        def _():
            down_grad(p)

        for s in range(3):

            @pl.when(p == s)
            def _():
                for side in range(2):
                    if s == 2:
                        dn_copy(0, 1 - side).wait_recv()
                        dn[2, side] = add(dn[2, side], dn_far[1 - side, 0])
                    dn_copy(s, side).start()

        @pl.when(p == 0)
        def _():
            for zp in range(chips):
                remote(
                    part.at[zp * 2 + (1 - c)], sib_part.at[zp], part_sib.at[zp],
                    part_sib_recv.at[zp], "expert", sibling,
                ).wait_recv()
                part[zp * 2 + c] = add(part[zp * 2 + c], sib_part[zp])

        @pl.when(jnp.logical_and(outer, p == 1))
        def _():
            part_copy(1).start()
            part_copy(2).start()

        pl.when(jnp.logical_and(inner, p == replicas - 2))(part_copy(2).start)

    @pl.when(inner)
    def _():
        part_copy(0).start()

    pl.when(outer)(part_copy(3).start)

    def gu_copy(s, side, n):
        to = jnp.where(side == 0, dx, dy)
        return remote(
            gu.at[s, side, n], gu_far.at[side, s, n], gu_send.at[s, side, n],
            gu_recv.at[side, s, n], "dp", to,
        )

    @pl.loop(0, 4 * replicas)
    def _(k):
        s = k // 4
        n = (k // 2) % 2
        side = k % 2
        lhs = rows[:, :, cols_of(s, side)].reshape(experts * count, half)
        gu[s, side, n] = lax.dot_general(
            lhs, back[:, pl.ds(pl.multiple_of(n * ff, ff), ff)], (((0,), (0,)), ((), ())),
            preferred_element_type=f32,
        ).astype(bf16)

        @pl.when(s == 2)
        def _():
            gu_copy(0, 1 - side, n).wait_recv()
            gu[2, side, n] = add(gu[2, side, n], gu_far[1 - side, 0, n])

        @pl.when(s < 3)
        def _():
            gu_copy(s, side, n).start()

    pl.when(inner)(part_copy(3).start)
    down_grad(replicas - 1)

    def total(own, one, two):
        return (own.astype(f32) + one.astype(f32) + two.astype(f32)).astype(bf16)

    def down_store(side):
        return pltpu.make_async_copy(
            dn.at[3, side], down_out.at[:, pl.ds(side * half, half)], out_sem.at[side]
        )

    for side in range(2):
        dn_copy(1, side).wait_recv()
        dn_copy(2, 1 - side).wait_recv()
        dn[3, side] = total(dn[3, side], dn_far[side, 1], dn_far[1 - side, 2])
        down_store(side).start()

    def far_copy(m):
        zp = at_chip(m)
        return remote(
            part.at[zp * 2 + c], far_part.at[zp], part_send.at[m], part_recv.at[zp], "expert",
            zp * 2 + c,
        )

    for m in range(chips):
        pl.when(zm != m)(far_copy(m).wait_recv)
    mixed = part[me].astype(f32)
    for q in range(1, chips):
        mixed = mixed + far_part[source(q)].astype(f32)
    part[me] = mixed.astype(bf16)
    mixed_store = pltpu.make_async_copy(part.at[me], combined, out_sem.at[2])
    mixed_store.start()

    def gu_store(side, n):
        return pltpu.make_async_copy(
            gu.at[3, side, n], (gate_out, up_out)[n].at[pl.ds(side * half, half)],
            out_sem.at[3 + 2 * n + side],
        )

    for n in range(2):
        for side in range(2):
            gu_copy(1, side, n).wait_recv()
            gu_copy(2, 1 - side, n).wait_recv()
            gu[3, side, n] = total(gu[3, side, n], gu_far[side, 1, n], gu_far[1 - side, 2, n])
            gu_store(side, n).start()

    own_to_sib.wait_send()
    for h in range(2):
        tok_own(1, h).wait_send()

        @pl.when(inner)
        def _():
            tok_own(0, h).wait_send()
            tok_hop(1, at_chip(0), h).wait_send()
            tok_hop(0, at_chip(2), h).wait_send()
            tok_hop(0, at_chip(3), h).wait_send()

    for p in range(replicas):
        cot_hop(1, p, z).wait_send()

        @pl.when(inner)
        def _():
            cot_hop(0, p, z).wait_send()
            cot_hop(1, p, at_chip(0)).wait_send()
            cot_hop(0, p, at_chip(2)).wait_send()
            cot_hop(0, p, at_chip(3)).wait_send()

    for r in range(1, experts):
        for k in range(2):
            route_copy(r, k).wait_send()
    for q in range(chips):
        zp = source(q)
        if q > 0:
            tok_to_sib(zp).wait_send()
        part_to_sib(zp).wait_send()
        for p in range(replicas):
            cot_to_sib(p, zp).wait_send()
        pl.when(zm != q)(part_copy(q).wait_send)
    for s in range(3):
        for side in range(2):
            dn_copy(s, side).wait_send()
            for n in range(2):
                gu_copy(s, side, n).wait_send()
    for side in range(2):
        down_store(side).wait()
        for n in range(2):
            gu_store(side, n).wait()
    mixed_store.wait()


def hand_on(*refs):
    arrays, outs, held, sems = refs[:4], refs[4:8], refs[8:12], refs[12]
    into = [pltpu.make_async_copy(arrays[k], held[k], sems.at[0, k]) for k in range(4)]
    back = [pltpu.make_async_copy(held[k], outs[k], sems.at[1, k]) for k in range(4)]
    for copy in into:
        copy.start()
    for k in range(4):
        into[k].wait()
        back[k].start()
    for copy in back:
        copy.wait()


def chain_local(tokens, expert_ids, probs, trade, gate_weight, up_weight, down_weight, out_grad):
    count, width = tokens.shape
    ff = gate_weight.shape[2]
    experts = lax.axis_size("expert")
    replicas = lax.axis_size("dp")
    chips = experts // 2
    share = width // replicas
    half = share // 2
    top = expert_ids.shape[1]
    bf16, f32 = jnp.bfloat16, jnp.float32
    dma = pltpu.SemaphoreType.DMA
    total = experts * count
    hbm = pl.BlockSpec(memory_space=pl.ANY)
    results = pl.pallas_call(
        layer_kernel,
        out_shape=(
            jax.ShapeDtypeStruct((count, width), bf16),
            jax.ShapeDtypeStruct((share, ff), bf16),
            jax.ShapeDtypeStruct((share, ff), bf16),
            jax.ShapeDtypeStruct((ff, share), bf16),
        ),
        in_specs=[hbm] * 4 + [pl.BlockSpec(memory_space=pltpu.SMEM)] + [hbm] * 3,
        out_specs=(hbm,) * 4,
        scratch_shapes=[
            pltpu.VMEM((experts, count, width), bf16),
            pltpu.VMEM((replicas, experts, count, share), bf16),
            pltpu.VMEM((experts, top, count), jnp.int32),
            pltpu.VMEM((experts, top, count), f32),
            pltpu.VMEM((width, ff), bf16),
            pltpu.VMEM((width, ff), bf16),
            pltpu.VMEM((ff, width), bf16),
            pltpu.VMEM((total, count), f32),
            pltpu.VMEM((total, ff), bf16),
            pltpu.VMEM((total, 2 * ff), bf16),
            pltpu.VMEM((total, ff), f32),
            pltpu.VMEM((total, share), bf16),
            pltpu.VMEM((experts, count, width), bf16),
            pltpu.VMEM((chips, count, width), bf16),
            pltpu.VMEM((chips, count, width), bf16),
            pltpu.VMEM((4, 2, 2, half, ff), bf16),
            pltpu.VMEM((2, 3, 2, half, ff), bf16),
            pltpu.VMEM((4, 2, ff, half), bf16),
            pltpu.VMEM((2, 3, ff, half), bf16),
            dma((6 + 2 * replicas,)),
            dma((7,)),
            dma((2, chips, 2)),
            dma((chips,)),
            dma((experts, 2)),
            dma((2, replicas, chips)),
            dma((replicas, chips)),
            dma((replicas, experts)),
            dma((2, experts)),
            dma((2, experts)),
            dma((chips,)),
            dma((chips,)),
            dma((chips,)),
            dma((chips,)),
            dma((3, 2, 2)),
            dma((2, 3, 2)),
            dma((3, 2)),
            dma((2, 3)),
        ],
        compiler_params=pltpu.CompilerParams(
            collective_id=0, has_side_effects=True, vmem_limit_bytes=67043328
        ),
    )(
        tokens, out_grad, expert_ids.T, probs.T, trade,
        gate_weight[0], up_weight[0], down_weight[0],
    )
    combined, gate, up, down = pl.pallas_call(
        hand_on,
        out_shape=[jax.ShapeDtypeStruct(r.shape, r.dtype) for r in results],
        in_specs=[hbm] * 4,
        out_specs=[hbm] * 4,
        scratch_shapes=[pltpu.VMEM(r.shape, r.dtype) for r in results] + [dma((2, 4))],
    )(*results)
    return combined, gate[None], up[None], down[None]


def local(tokens, expert_ids, *rest):
    experts, replicas = lax.axis_size("expert"), lax.axis_size("dp")
    capacity = 5 * tokens.shape[0] * expert_ids.shape[1] // (4 * experts)
    if tokens.shape[0] <= 2 * capacity and experts == 8 and replicas == 4:
        return chain_local(tokens, expert_ids, *rest)
    return sparse_local(tokens, expert_ids, *rest)


def solution(mesh):
    return jax.shard_map(
        local,
        mesh=mesh,
        in_specs=(
            P(("dp", "expert"), None),
            P(("dp", "expert"), None),
            P(("dp", "expert"), None),
            P(),
            P("expert", None, None),
            P("expert", None, None),
            P("expert", None, None),
            P(("dp", "expert"), None),
        ),
        out_specs=(
            P(("dp", "expert"), None),
            P("expert", "dp", None),
            P("expert", "dp", None),
            P("expert", None, "dp"),
        ),
        check_vma=False,
    )
```

```python
import functools
import jax
import jax.numpy as jnp
from jax import lax
from jax.experimental import pallas as pl
from jax.experimental.pallas import tpu as pltpu
from jax.sharding import PartitionSpec as P


def sparse_local(tokens, expert_ids, probs, trade, gate_weight, up_weight, down_weight, out_grad):
    tok_count, model_width = tokens.shape
    top_count = expert_ids.shape[1]
    hidden_width = gate_weight.shape[2]
    experts = lax.axis_size("expert")
    capacity = 5 * tok_count * top_count // (4 * experts)
    halfway = experts // 2
    chosen = expert_ids.reshape(-1)
    numbers = jnp.arange(experts, dtype=jnp.int32)
    onehot = (chosen[:, None] == numbers[None, :]).astype(jnp.int32)
    earlier = jnp.cumsum(onehot, axis=0) - onehot
    slots = chosen * capacity + jnp.sum(earlier * onehot, axis=1)
    owners = jnp.where(trade[numbers % halfway] == 1, jnp.bitwise_xor(numbers, halfway), numbers)
    pair_tokens = jnp.arange(chosen.shape[0], dtype=jnp.int32) // top_count
    send_rows = (
        jnp.zeros((experts * capacity, model_width), jnp.bfloat16)
        .at[slots]
        .set(tokens[pair_tokens])
    )
    send_rows = send_rows.reshape(experts, capacity, model_width)
    out_pairs = (probs[:, :, None] * out_grad[:, None, :].astype(jnp.float32)).astype(jnp.bfloat16)
    send_grads = (
        jnp.zeros((experts * capacity, model_width), jnp.bfloat16)
        .at[slots]
        .set(out_pairs.reshape(-1, model_width))
    )
    send_grads = send_grads.reshape(experts, capacity, model_width)
    send_rows = send_rows[owners]
    send_grads = send_grads[owners]
    w_gate = gate_weight[0]
    w_up = up_weight[0]
    w_down = down_weight[0]
    arrived = lax.all_to_all(send_rows, "expert", split_axis=0, concat_axis=0, tiled=True)
    lead = arrived.shape[:2]
    flat_rows = arrived.reshape(-1, model_width)
    gate_act = jnp.dot(flat_rows, w_gate, preferred_element_type=jnp.float32)
    up_act = jnp.dot(flat_rows, w_up, preferred_element_type=jnp.float32)
    forward_hidden = (gate_act * jax.nn.sigmoid(gate_act) * up_act).astype(jnp.bfloat16)
    expert_out = jnp.dot(forward_hidden, w_down, preferred_element_type=jnp.float32).astype(
        jnp.bfloat16
    )
    arrived, expert_out, hidden, gate_act, up_act = (
        arrived,
        expert_out.reshape(lead + (model_width,)),
        forward_hidden.reshape(lead + (hidden_width,)),
        gate_act.reshape(lead + (hidden_width,)),
        up_act.reshape(lead + (hidden_width,)),
    )
    returned = lax.all_to_all(expert_out, "expert", split_axis=0, concat_axis=0, tiled=True)
    out_rows = lax.all_to_all(send_grads, "expert", split_axis=0, concat_axis=0, tiled=True)
    returned = returned[owners]
    picked = returned.reshape(-1, model_width)[slots].reshape(tok_count, top_count, model_width)
    combined = jnp.sum(probs[:, :, None] * picked.astype(jnp.float32), axis=1).astype(jnp.bfloat16)
    expert_rows = arrived.reshape(-1, model_width)
    out_rows = out_rows.reshape(-1, model_width)
    hidden = hidden.reshape(-1, hidden_width)
    gate_act = gate_act.reshape(-1, hidden_width)
    up_act = up_act.reshape(-1, hidden_width)
    hidden_grad = lax.dot_general(
        out_rows, w_down, (((1,), (1,)), ((), ())), preferred_element_type=jnp.float32
    )
    sigma = jax.nn.sigmoid(gate_act)
    gate_back = (hidden_grad * up_act * (sigma * (1.0 + gate_act * (1.0 - sigma)))).astype(
        jnp.bfloat16
    )
    up_back = (hidden_grad * (gate_act * sigma)).astype(jnp.bfloat16)
    both_back = jnp.concatenate([gate_back, up_back], axis=1)
    first = lax.dot_general(
        expert_rows, both_back, (((0,), (0,)), ((), ())), preferred_element_type=jnp.float32
    )
    second = lax.dot_general(
        out_rows, hidden, (((0,), (0,)), ((), ())), preferred_element_type=jnp.float32
    )
    summed = lax.psum_scatter(
        jnp.concatenate([first, second], axis=1).astype(jnp.bfloat16),
        "dp",
        scatter_dimension=0,
        tiled=True,
    )
    gate_part = summed[:, :hidden_width]
    up_part = summed[:, hidden_width : 2 * hidden_width]
    down_part = summed[:, 2 * hidden_width :].T
    return (combined, gate_part[None], up_part[None], down_part[None])


def layer_kernel(
    tokens, grads, ids, probs, trade, wg_hbm, wu_hbm, wd_hbm,
    combined, gate_out, up_out, down_out,
    rows, cots, all_ids, all_probs, wg, wu, wd, wcol, hidden, back, acc, pairs, part, sib_part, far_part,
    gu, gu_far, dn, dn_far, via,
    load_sem, out_sem, tok_send, tok_sib, tok_recv, cot_send, cot_sib, cot_recv, wt_send, wt_recv,
    part_sib, part_sib_recv, part_send, part_recv, gu_send, gu_recv, dn_send, dn_recv,
    via_send, via_recv, rest_send, rest_recv,
):
    f32 = jnp.float32
    bf16 = jnp.bfloat16
    experts = lax.axis_size("expert")
    chips = experts // 2
    last = chips - 1
    replicas = lax.axis_size("dp")
    count, width = tokens.shape
    share = width // replicas
    half = share // 2
    ff = wg.shape[1]
    pair = 2 * count
    me = lax.axis_index("expert")
    z = me // 2
    c = me % 2
    d = lax.axis_index("dp")
    dx = (d // 2) * 2 + (1 - d % 2)
    dy = (1 - d // 2) * 2 + d % 2
    dd = 3 - d
    upper = z // (chips // 2)
    zm = z * (1 - upper) + (last - z) * upper
    sibling = z * 2 + (1 - c)
    inner = zm == 1
    outer = zm == 0

    def at_chip(m):
        return m * (1 - upper) + (last - m) * upper

    def source(q):
        return at_chip(jnp.where(q == 0, zm, jnp.where(q == 1, 1 - zm, q)))

    def cols_of(s, side):
        to = jnp.where(side == 0, dx, dy)
        owner = jnp.where(s == 0, dd, jnp.where(s == 3, d, to))
        h = jnp.where(s == 2, 1 - side, side)
        return pl.ds(pl.multiple_of(owner * share + h * half, half), half)

    def remote(src, dst, ssem, rsem, axis, to):
        device = to if axis is None else {axis: to}
        return pltpu.make_async_remote_copy(
            src_ref=src, dst_ref=dst, send_sem=ssem, recv_sem=rsem,
            device_id=device, device_id_type=pl.DeviceIdType.MESH,
        )

    loads = [
        pltpu.make_async_copy(wg_hbm, wg, load_sem.at[0]),
        pltpu.make_async_copy(wu_hbm, wu, load_sem.at[1]),
        pltpu.make_async_copy(wd_hbm, wd, load_sem.at[2]),
        pltpu.make_async_copy(tokens, rows.at[me], load_sem.at[3]),
        pltpu.make_async_copy(ids, all_ids.at[me], load_sem.at[4]),
        pltpu.make_async_copy(probs, all_probs.at[me], load_sem.at[5]),
    ]

    def cot_load(p, side):
        return pltpu.make_async_copy(
            grads.at[:, cols_of(p, side)], cots.at[p, me, :, pl.ds(side * half, half)],
            load_sem.at[6 + 2 * p + side],
        )

    for load in loads[3:]:
        load.start()
    for p in range(replicas):
        for side in range(2):
            cot_load(p, side).start()
    for load in loads[:3]:
        load.start()

    barrier = pltpu.get_barrier_semaphore()
    for r in range(1, experts):
        pl.semaphore_signal(
            barrier, inc=1, device_id={"expert": (me + r) % experts},
            device_id_type=pl.DeviceIdType.MESH,
        )
    for to in (dx, dy):
        pl.semaphore_signal(
            barrier, inc=1, device_id={"dp": to}, device_id_type=pl.DeviceIdType.MESH
        )
        pl.semaphore_signal(
            barrier, inc=1, device_id={"dp": to, "expert": at_chip(1 - zm) * 2 + c},
            device_id_type=pl.DeviceIdType.MESH,
        )
    pl.semaphore_wait(barrier, experts + 3)

    to_chip = (at_chip(0) * 2 + c, at_chip(zm + 1) * 2 + c)
    rhalf = count // 2

    def tok_own(way, h):
        part_rows = pl.ds(h * rhalf, rhalf)
        return remote(
            tokens.at[part_rows], rows.at[me, part_rows], tok_send.at[way, z, h],
            tok_recv.at[me, h], "expert", to_chip[way],
        )

    def tok_hop(way, zp, h):
        ref = rows.at[zp * 2 + c, pl.ds(h * rhalf, rhalf)]
        return remote(
            ref, ref, tok_send.at[way, zp, h], tok_recv.at[zp * 2 + c, h], "expert", to_chip[way]
        )

    def tok_to_sib(zp):
        ref = rows.at[zp * 2 + c]
        return remote(ref, ref, tok_sib.at[zp], tok_recv.at[zp * 2 + c, 0], "expert", sibling)

    def cot_hop(way, p, zp):
        ref = cots.at[p, zp * 2 + c]
        return remote(
            ref, ref, cot_send.at[way, p, zp], cot_recv.at[p, zp * 2 + c], "expert", to_chip[way]
        )

    def cot_to_sib(p, zp):
        ref = cots.at[p, zp * 2 + c]
        return remote(ref, ref, cot_sib.at[p, zp], cot_recv.at[p, zp * 2 + c], "expert", sibling)

    def route_copy(r, k):
        ref, dst = ((ids, all_ids), (probs, all_probs))[k]
        return remote(
            ref, dst.at[me], wt_send.at[k, r], wt_recv.at[k, me], "expert", (me + r) % experts
        )

    def route_from(slot, k):
        ref, dst = ((ids, all_ids), (probs, all_probs))[k]
        return remote(
            ref, dst.at[slot], wt_send.at[k, 1], wt_recv.at[k, slot], "expert", sibling
        )

    own_to_sib = remote(
        tokens, rows.at[me], tok_sib.at[z], tok_recv.at[me, 0], "expert", sibling
    )

    for r in range(1, experts):
        for k in range(2):
            route_copy(r, k).start()
    own_to_sib.start()
    for h in range(2):
        tok_own(1, h).start()
        pl.when(inner)(tok_own(0, h).start)
    for p in range(replicas):
        for side in range(2):
            cot_load(p, side).wait()
        cot_to_sib(p, z).start()

        pl.when(outer)(cot_hop(1, p, z).start)

    def part_to_sib(zp):
        return remote(
            part.at[zp * 2 + (1 - c)], sib_part.at[zp], part_sib.at[zp], part_sib_recv.at[zp],
            "expert", sibling,
        )

    eye = lax.broadcasted_iota(jnp.int32, (count, count), 0) == lax.broadcasted_iota(
        jnp.int32, (count, count), 1
    )

    halfway = experts // 2
    swapped = jnp.where(me < halfway, me + halfway, me - halfway)
    name = jnp.where(trade[me % halfway] == 1, swapped, me)

    def weight_column(slot):
        row = jnp.sum(
            jnp.where(all_ids[slot] == name, all_probs[slot], 0.0), axis=0, keepdims=True
        )
        row = jnp.broadcast_to(row, (count, count))
        column = jnp.sum(jnp.where(eye, row, 0.0), axis=1, keepdims=True)
        wcol[pl.ds(pl.multiple_of(slot * count, count), count), :] = jnp.broadcast_to(
            column, (count, wcol.shape[1])
        )

    for load in loads[3:]:
        load.wait()

    @pl.loop(0, chips)
    def _(q):
        zp = source(q)
        slot = zp * 2 + c

        @pl.when(jnp.logical_and(q > 0, jnp.logical_not(jnp.logical_and(inner, q == 2))))
        def _():
            @pl.when(jnp.logical_not(jnp.logical_and(inner, q == 3)))
            def _():
                tok_hop(0, zp, 0).wait_recv()

                @pl.when(inner)
                def _():
                    tok_hop(1, zp, 0).start()
                    tok_hop(0, at_chip(2), 0).wait_recv()
                    tok_hop(0, at_chip(2), 0).start()

            tok_hop(0, zp, 1).wait_recv()

            @pl.when(jnp.logical_and(inner, q == 1))
            def _():
                tok_hop(1, zp, 1).start()
                tok_hop(0, at_chip(2), 1).wait_recv()
                tok_hop(0, at_chip(2), 1).start()
                tok_to_sib(at_chip(2)).start()

            @pl.when(jnp.logical_and(inner, q == 3))
            def _():
                tok_hop(0, zp, 1).start()
                cot_hop(0, 0, z).start()

            tok_to_sib(zp).start()

        @pl.when(jnp.logical_and(inner, q == 2))
        def _():
            for p in range(replicas):
                cot_hop(1, p, z).start()
                cot_hop(1, p, at_chip(0)).wait_recv()
                cot_hop(1, p, at_chip(0)).start()
            tok_hop(0, at_chip(3), 0).wait_recv()
            tok_hop(0, at_chip(3), 0).start()

        @pl.when(q == 0)
        def _():
            for k in range(2):
                route_from(sibling, k).wait_recv()
            weight_column(me)
            weight_column(sibling)
            for load in loads[:3]:
                load.wait()

        @pl.when(q > 0)
        def _():
            for k in range(2):
                for part_of in range(2):
                    route_from(zp * 2 + k, part_of).wait_recv()
                weight_column(zp * 2 + k)

        remote(
            rows.at[zp * 2 + 1 - c], rows.at[zp * 2 + 1 - c], tok_sib.at[zp],
            tok_recv.at[zp * 2 + 1 - c, 0], "expert", sibling,
        ).wait_recv()
        where = pl.ds(pl.multiple_of(zp * pair, pair), pair)
        x = rows[pl.ds(zp * 2, 2)].reshape(pair, width)
        tile = ff // 3

        @pl.loop(0, 3)
        def _(n):
            cols = pl.ds(pl.multiple_of(n * tile, tile), tile)
            g = jnp.dot(x, wg[:, cols], preferred_element_type=f32)
            u = jnp.dot(x, wu[:, cols], preferred_element_type=f32)
            sigma = jax.nn.sigmoid(g)
            silu = g * sigma
            hidden[where, cols] = (silu * u).astype(bf16)
            back[where, cols] = (u * (sigma * (1.0 + g * (1.0 - sigma)))).astype(bf16)
            back[where, pl.ds(pl.multiple_of(ff + n * tile, tile), tile)] = silu.astype(bf16)

        @pl.loop(0, replicas)
        def _(n):
            cols = pl.ds(pl.multiple_of(n * share, share), share)
            o = jnp.dot(hidden[where, :], wd[:, cols], preferred_element_type=f32)
            o = (o * wcol[where, 0:1]).astype(bf16)
            part[zp * 2, :, cols] = o[:count]
            part[zp * 2 + 1, :, cols] = o[count:]

        part_to_sib(zp).start()

    def part_copy(m):
        zp = at_chip(m)
        return remote(
            part.at[zp * 2 + c], far_part.at[z], part_send.at[m], part_recv.at[z], "expert",
            zp * 2 + c,
        )

    def dn_copy(s, side):
        return remote(
            dn.at[s, side], dn_far.at[side, s], dn_send.at[s, side], dn_recv.at[side, s], "dp",
            (dx, dy)[side],
        )

    def down_grad(p):
        for side in range(2):
            dn[p, side] = lax.dot_general(
                hidden[...], pairs[:, side * half:(side + 1) * half], (((0,), (0,)), ((), ())),
                preferred_element_type=f32,
            ).astype(bf16)

    def add(a, b):
        return (a.astype(f32) + b.astype(f32)).astype(bf16)

    @pl.loop(0, replicas)
    def _(p):
        def use(q):
            zp = source(q)
            other = zp * 2 + 1 - c
            remote(
                cots.at[p, other], cots.at[p, other], cot_sib.at[p, zp], cot_recv.at[p, other],
                "expert", sibling,
            ).wait_recv()
            where = pl.ds(pl.multiple_of(zp * pair, pair), pair)
            both = cots[p, pl.ds(zp * 2, 2)].reshape(pair, share)
            scaled = (wcol[where, 0:1] * both.astype(f32)).astype(bf16)
            pairs[where, :] = scaled
            more = lax.dot_general(
                scaled,
                jnp.concatenate([wd[:, cols_of(p, 0)], wd[:, cols_of(p, 1)]], axis=1),
                (((1,), (1,)), ((), ())), preferred_element_type=f32,
            )
            total = jnp.where(p == 0, more, acc[where, :] + more)
            acc[where, :] = total

            @pl.when(p == replicas - 1)
            def _():
                for n in range(2):
                    cols = slice(n * ff, (n + 1) * ff)
                    back[where, cols] = (acc[where, :] * back[where, cols].astype(f32)).astype(bf16)

        for q in range(chips):
            zp = source(q)
            if q == 1:
                pl.when(outer)(cot_hop(0, p, zp).wait_recv)
            elif q > 1:
                cot_hop(0, p, zp).wait_recv()
                pl.when(inner)(cot_hop(0, p, zp).start)
            if q > 0:
                cot_to_sib(p, zp).start()
            if q == last:

                @pl.when(jnp.logical_and(inner, p < replicas - 1))
                def _():
                    cot_hop(0, p + 1, z).start()

            if q > 0:
                use(q - 1)
        use(last)

        @pl.when(p < replicas - 1)
        def _():
            down_grad(p)

        for s in range(3):

            @pl.when(p == s)
            def _():
                for side in range(2):
                    if s == 2:
                        dn_copy(0, 1 - side).wait_recv()
                        dn[2, side] = add(dn[2, side], dn_far[1 - side, 0])
                    dn_copy(s, side).start()

        @pl.when(p == 0)
        def _():
            for zp in range(chips):
                remote(
                    part.at[zp * 2 + (1 - c)], sib_part.at[zp], part_sib.at[zp],
                    part_sib_recv.at[zp], "expert", sibling,
                ).wait_recv()
                part[zp * 2 + c] = add(part[zp * 2 + c], sib_part[zp])

        @pl.when(jnp.logical_and(outer, p == 1))
        def _():
            part_copy(1).start()
            part_copy(2).start()

        pl.when(jnp.logical_and(inner, p == replicas - 2))(part_copy(2).start)

    pl.when(inner)(part_copy(0).start)

    detour = via.shape[1]
    rest = pl.ds(half - detour, detour)

    def gu_copy(s, side, n, short=False):
        to = jnp.where(side == 0, dx, dy)
        if short:
            kept = pl.ds(0, half - detour)
            return remote(
                gu.at[s, side, n, kept], gu_far.at[side, s, n, kept], gu_send.at[s, side, n],
                gu_recv.at[side, s, n], "dp", to,
            )
        return remote(
            gu.at[s, side, n], gu_far.at[side, s, n], gu_send.at[s, side, n],
            gu_recv.at[side, s, n], "dp", to,
        )

    def rest_copy(side):
        return remote(
            gu.at[1, side, 1, rest], gu_far.at[side, 1, 1, rest], rest_send.at[side],
            rest_recv.at[side], "dp", jnp.where(side == 0, dx, dy),
        )

    def via_copy(side):
        to = jnp.where(side == 0, dx, dy)
        return remote(
            gu.at[1, side, 1, rest], via.at[side], rest_send.at[side], via_recv.at[side], None,
            {"dp": to, "expert": at_chip(1) * 2 + c},
        )

    def via_hop(side):
        return remote(
            via.at[side], gu_far.at[side, 1, 1, rest], via_send.at[side], rest_recv.at[side],
            "expert", at_chip(0) * 2 + c,
        )

    pl.when(outer)(part_copy(3).start)

    @pl.loop(0, 4 * replicas)
    def _(k):
        s = k // 4
        n = (k // 2) % 2
        side = k % 2
        lhs = rows[:, :, cols_of(s, side)].reshape(experts * count, half)
        gu[s, side, n] = lax.dot_general(
            lhs, back[:, pl.ds(pl.multiple_of(n * ff, ff), ff)], (((0,), (0,)), ((), ())),
            preferred_element_type=f32,
        ).astype(bf16)

        @pl.when(s == 2)
        def _():
            gu_copy(0, 1 - side, n).wait_recv()
            gu[2, side, n] = add(gu[2, side, n], gu_far[1 - side, 0, n])

        apart = jnp.logical_and(s == 1, n == 1)

        @pl.when(jnp.logical_and(s < 3, jnp.logical_not(apart)))
        def _():
            gu_copy(s, side, n).start()

        @pl.when(apart)
        def _():
            pl.when(outer)(via_copy(side).start)
            gu_copy(1, side, 1, True).start()
            pl.when(inner)(rest_copy(side).start)

    pl.when(inner)(part_copy(3).start)
    down_grad(replicas - 1)

    @pl.when(inner)
    def _():
        for side in range(2):
            via_copy(side).wait_recv()
            via_hop(side).start()

    def total(own, one, two):
        return (own.astype(f32) + one.astype(f32) + two.astype(f32)).astype(bf16)

    def down_store(side):
        return pltpu.make_async_copy(
            dn.at[3, side], down_out.at[:, pl.ds(side * half, half)], out_sem.at[side]
        )

    for side in range(2):
        dn_copy(1, side).wait_recv()
        dn_copy(2, 1 - side).wait_recv()
        dn[3, side] = total(dn[3, side], dn_far[side, 1], dn_far[1 - side, 2])
        down_store(side).start()

    def far_copy(m):
        zp = at_chip(m)
        return remote(
            part.at[zp * 2 + c], far_part.at[zp], part_send.at[m], part_recv.at[zp], "expert",
            zp * 2 + c,
        )

    for m in range(chips):
        pl.when(zm != m)(far_copy(m).wait_recv)
    mixed = part[me].astype(f32)
    for q in range(1, chips):
        mixed = mixed + far_part[source(q)].astype(f32)
    part[me] = mixed.astype(bf16)
    mixed_store = pltpu.make_async_copy(part.at[me], combined, out_sem.at[2])
    mixed_store.start()

    def gu_store(side, n):
        return pltpu.make_async_copy(
            gu.at[3, side, n], (gate_out, up_out)[n].at[pl.ds(side * half, half)],
            out_sem.at[3 + 2 * n + side],
        )

    for n in range(2):
        for side in range(2):
            gu_copy(1, side, n, n == 1).wait_recv()
            if n == 1:
                rest_copy(side).wait_recv()
            gu_copy(2, 1 - side, n).wait_recv()
            gu[3, side, n] = total(gu[3, side, n], gu_far[side, 1, n], gu_far[1 - side, 2, n])
            gu_store(side, n).start()

    own_to_sib.wait_send()
    for h in range(2):
        tok_own(1, h).wait_send()

        @pl.when(inner)
        def _():
            tok_own(0, h).wait_send()
            tok_hop(1, at_chip(0), h).wait_send()
            tok_hop(0, at_chip(2), h).wait_send()
            tok_hop(0, at_chip(3), h).wait_send()

    for p in range(replicas):
        cot_hop(1, p, z).wait_send()

        @pl.when(inner)
        def _():
            cot_hop(0, p, z).wait_send()
            cot_hop(1, p, at_chip(0)).wait_send()
            cot_hop(0, p, at_chip(2)).wait_send()
            cot_hop(0, p, at_chip(3)).wait_send()

    for r in range(1, experts):
        for k in range(2):
            route_copy(r, k).wait_send()
    for q in range(chips):
        zp = source(q)
        if q > 0:
            tok_to_sib(zp).wait_send()
        part_to_sib(zp).wait_send()
        for p in range(replicas):
            cot_to_sib(p, zp).wait_send()
        pl.when(zm != q)(part_copy(q).wait_send)
    for s in range(3):
        for side in range(2):
            dn_copy(s, side).wait_send()
            for n in range(2):
                gu_copy(s, side, n, (s, n) == (1, 1)).wait_send()
        if s < 2:
            pl.when(inner)(via_hop(s).wait_send)
            rest_copy(s).wait_send()
    for side in range(2):
        down_store(side).wait()
        for n in range(2):
            gu_store(side, n).wait()
    mixed_store.wait()


def hand_on(*refs):
    arrays, outs, held, sems = refs[:4], refs[4:8], refs[8:12], refs[12]
    into = [pltpu.make_async_copy(arrays[k], held[k], sems.at[0, k]) for k in range(4)]
    back = [pltpu.make_async_copy(held[k], outs[k], sems.at[1, k]) for k in range(4)]
    for copy in into:
        copy.start()
    for k in range(4):
        into[k].wait()
        back[k].start()
    for copy in back:
        copy.wait()


def chain_local(tokens, expert_ids, probs, trade, gate_weight, up_weight, down_weight, out_grad):
    count, width = tokens.shape
    ff = gate_weight.shape[2]
    experts = lax.axis_size("expert")
    replicas = lax.axis_size("dp")
    chips = experts // 2
    share = width // replicas
    half = share // 2
    top = expert_ids.shape[1]
    bf16, f32 = jnp.bfloat16, jnp.float32
    dma = pltpu.SemaphoreType.DMA
    total = experts * count
    hbm = pl.BlockSpec(memory_space=pl.ANY)
    results = pl.pallas_call(
        layer_kernel,
        out_shape=(
            jax.ShapeDtypeStruct((count, width), bf16),
            jax.ShapeDtypeStruct((share, ff), bf16),
            jax.ShapeDtypeStruct((share, ff), bf16),
            jax.ShapeDtypeStruct((ff, share), bf16),
        ),
        in_specs=[hbm] * 4 + [pl.BlockSpec(memory_space=pltpu.SMEM)] + [hbm] * 3,
        out_specs=(hbm,) * 4,
        scratch_shapes=[
            pltpu.VMEM((experts, count, width), bf16),
            pltpu.VMEM((replicas, experts, count, share), bf16),
            pltpu.VMEM((experts, top, count), jnp.int32),
            pltpu.VMEM((experts, top, count), f32),
            pltpu.VMEM((width, ff), bf16),
            pltpu.VMEM((width, ff), bf16),
            pltpu.VMEM((ff, width), bf16),
            pltpu.VMEM((total, count), f32),
            pltpu.VMEM((total, ff), bf16),
            pltpu.VMEM((total, 2 * ff), bf16),
            pltpu.VMEM((total, ff), f32),
            pltpu.VMEM((total, share), bf16),
            pltpu.VMEM((experts, count, width), bf16),
            pltpu.VMEM((chips, count, width), bf16),
            pltpu.VMEM((chips, count, width), bf16),
            pltpu.VMEM((4, 2, 2, half, ff), bf16),
            pltpu.VMEM((2, 3, 2, half, ff), bf16),
            pltpu.VMEM((4, 2, ff, half), bf16),
            pltpu.VMEM((2, 3, ff, half), bf16),
            pltpu.VMEM((2, half // 2, ff), bf16),
            dma((6 + 2 * replicas,)),
            dma((7,)),
            dma((2, chips, 2)),
            dma((chips,)),
            dma((experts, 2)),
            dma((2, replicas, chips)),
            dma((replicas, chips)),
            dma((replicas, experts)),
            dma((2, experts)),
            dma((2, experts)),
            dma((chips,)),
            dma((chips,)),
            dma((chips,)),
            dma((chips,)),
            dma((3, 2, 2)),
            dma((2, 3, 2)),
            dma((3, 2)),
            dma((2, 3)),
            dma((2,)),
            dma((2,)),
            dma((2,)),
            dma((2,)),
        ],
        compiler_params=pltpu.CompilerParams(
            collective_id=0, has_side_effects=True, vmem_limit_bytes=67043328
        ),
    )(
        tokens, out_grad, expert_ids.T, probs.T, trade,
        gate_weight[0], up_weight[0], down_weight[0],
    )
    combined, gate, up, down = pl.pallas_call(
        hand_on,
        out_shape=[jax.ShapeDtypeStruct(r.shape, r.dtype) for r in results],
        in_specs=[hbm] * 4,
        out_specs=[hbm] * 4,
        scratch_shapes=[pltpu.VMEM(r.shape, r.dtype) for r in results] + [dma((2, 4))],
    )(*results)
    return combined, gate[None], up[None], down[None]


def local(tokens, expert_ids, *rest):
    experts, replicas = lax.axis_size("expert"), lax.axis_size("dp")
    capacity = 5 * tokens.shape[0] * expert_ids.shape[1] // (4 * experts)
    if tokens.shape[0] <= 2 * capacity and experts == 8 and replicas == 4:
        return chain_local(tokens, expert_ids, *rest)
    return sparse_local(tokens, expert_ids, *rest)


def solution(mesh):
    return jax.shard_map(
        local,
        mesh=mesh,
        in_specs=(
            P(("dp", "expert"), None),
            P(("dp", "expert"), None),
            P(("dp", "expert"), None),
            P(),
            P("expert", None, None),
            P("expert", None, None),
            P("expert", None, None),
            P(("dp", "expert"), None),
        ),
        out_specs=(
            P(("dp", "expert"), None),
            P("expert", "dp", None),
            P("expert", "dp", None),
            P("expert", None, "dp"),
        ),
        check_vma=False,
    )
```
